256 devices in a mesh: dp: 16 (over z_lo, x), seq: 16 (over z_hi, y, core).
Axes of the slice: x: 4, y: 4, z: 8 (z_hi: 2, z_lo: 4; z = z_hi * 4 + z_lo), core: 2. Of those that a mesh axis runs over, the one named last changes fastest.
Arguments:
- frames: bfloat16 [16, 4096, 1280], P('dp', 'seq'), may hold values from -6 to 6
- live: int32 [16, 4096], P('dp', 'seq'), may hold values from 0 to 1
- norm_gain: float32 [1280], replicated, may hold values from 0.25 to 1.75
- w_qkv: bfloat16 [1280, 1920], P('dp')
- w_out: bfloat16 [640, 1280], P('dp'), may hold values from -0.25 to 0.25
- cotangent: bfloat16 [16, 4096, 1280], P('dp', 'seq'), may hold values from -6 to 6
Outputs:
- grad_frames: bfloat16 [16, 4096, 1280], P('dp', 'seq')
- grad_qkv: float32 [1280, 1920], P('dp', 'seq')
- grad_out: float32 [640, 1280], P('dp', 'seq')
The draws below stay inside these ranges and needn't reach their ends.
All inputs are finite; a program needn't handle non-finite values.
Results may differ from the reference program's by a relative error of at most 0.0095.
Values may be sent and summed in bfloat16 or wider, within the bound.
No kernel may reach another device: no remote copies, remote signals or barrier semaphores. Data moves between devices by JAX's collectives and lax.ppermute only.
A program may use at most 64 MiB of HBM per device.

```python
import math
import jax
import jax.numpy as jnp
from jax import lax

D = 1280
HEADS = 10
HEAD_DIM = 64
WIN = 512
FRAMES_DEV = 256
INNER = 640
SEQS = 16
FRAMES = 4096


def draw_live(key, part):
    level_key, frame_key = jax.random.split(key)
    run_count = FRAMES // FRAMES_DEV
    levels = jax.random.randint(level_key, (SEQS, run_count, 1), 0, 5)
    rolls = jax.random.randint(frame_key, (SEQS, run_count, FRAMES_DEV), 0, 4)
    return (rolls < levels).astype(jnp.int32).reshape(SEQS, FRAMES)


def draw_w_qkv(key, part):
    drawn = jax.random.normal(key, (D, 3 * INNER), jnp.float32) / math.sqrt(D)
    return drawn.astype(jnp.bfloat16)


def shard_levels(rng, dims, pieces, least, largest):
    def one(dim, blocks):
        draws = jax.random.uniform(jax.random.fold_in(jax.random.fold_in(rng, 6), dim), (blocks,), jnp.float32, least / len(pieces), largest / len(pieces))
        return jnp.repeat(jnp.exp(draws), dims[dim] // blocks).reshape((-1,) + (1,) * (len(dims) - dim - 1))

    level = one(*pieces[0])
    for cut in pieces[1:]:
        level = level * one(*cut)
    return level


def noise(own_key, extent, width, most, pieces=(), held_as=jnp.bfloat16):
    array = width * jax.random.normal(own_key, extent, jnp.float32)
    if pieces:
        array = array * shard_levels(own_key, extent, pieces, -0.22, 0.18)
    return jnp.clip(array, -most, most).astype(held_as)


def setup_inputs(seed: int = 0) -> dict:
    streams_of = jax.random.split(jax.random.key(seed), 7)
    return {
        "frames": noise(streams_of[0], (SEQS, FRAMES, D), 1.0, 6.0, ((0, 16), (1, 16))),
        "live": draw_live(jax.random.fold_in(streams_of[6], 71), 0),
        "norm_gain": jnp.clip(1.0 + 0.15 * jax.random.normal(streams_of[2], (D,), jnp.float32), 0.25, 1.75),
        "w_qkv": draw_w_qkv(jax.random.fold_in(streams_of[6], 71), 0),
        "w_out": noise(streams_of[4], (INNER, D), INNER ** -0.5, 0.25, ((0, 16),)),
        "cotangent": noise(streams_of[5], (SEQS, FRAMES, D), 1.0, 6.0, ((0, 16), (1, 16))),
    }


EPS = 1e-05
NEG = -1e+30

def norm_rows(values_in):
    average = lax.optimization_barrier(jnp.mean(values_in, axis=-1, keepdims=True))
    centred = values_in - average
    inverse = lax.rsqrt(lax.optimization_barrier(jnp.mean(centred * centred, axis=-1, keepdims=True)) + EPS)
    return (centred * inverse, inverse)

def block_terms(query_blk, key_blk, value_blk, grad_blk, allowed, query_live):
    length = query_blk.shape[0]
    key_span = key_blk.shape[0]
    score_scale = 1.0 / math.sqrt(HEAD_DIM)
    query_heads = query_blk.reshape(length, HEADS, HEAD_DIM).astype(jnp.float32)
    key_heads = key_blk.reshape(key_span, HEADS, HEAD_DIM).astype(jnp.float32)
    value_heads = value_blk.reshape(key_span, HEADS, HEAD_DIM).astype(jnp.float32)
    grad_heads = grad_blk.reshape(length, HEADS, HEAD_DIM).astype(jnp.float32)
    scores = jnp.einsum('bhd,shd->hbs', query_heads, key_heads) * score_scale
    scores = jnp.where(allowed[None], scores, NEG)
    row_peak = lax.optimization_barrier(jnp.max(scores, axis=-1, keepdims=True))
    exponent = jnp.exp(scores - row_peak)
    probabilities = exponent / lax.optimization_barrier(jnp.sum(exponent, axis=-1, keepdims=True))
    probs_b = lax.optimization_barrier(probabilities.astype(jnp.bfloat16)).astype(jnp.float32)
    mixed = jnp.einsum('hbs,shd->bhd', probs_b, value_heads) * query_live[:, None, None]
    attended = mixed.astype(jnp.bfloat16)
    attended_f = lax.optimization_barrier(attended).astype(jnp.float32)
    row_delta = lax.optimization_barrier(jnp.sum(grad_heads * attended_f, axis=-1))
    grad_probs = jnp.einsum('bhd,shd->hbs', grad_heads, value_heads)
    grad_scores = probabilities * (grad_probs - jnp.transpose(row_delta)[:, :, None]) * score_scale
    grad_scores = lax.optimization_barrier(grad_scores.astype(jnp.bfloat16)).astype(jnp.float32)
    grad_query = jnp.einsum('hbs,shd->bhd', grad_scores, key_heads)
    grad_key = jnp.einsum('hbs,bhd->shd', grad_scores, query_heads)
    grad_value = jnp.einsum('hbs,bhd->shd', probs_b, grad_heads)
    return (attended.reshape(length, INNER), grad_query.reshape(length, INNER), grad_key.reshape(key_span, INNER), grad_value.reshape(key_span, INNER))

def sequence_terms(query, keys, values, grad_att, live_row):
    block_rows = min(FRAMES_DEV, 512)
    block_count = FRAMES // block_rows
    key_span = block_rows + 2 * WIN
    padded_keys = jnp.pad(keys, ((WIN, WIN), (0, 0)))
    padded_values = jnp.pad(values, ((WIN, WIN), (0, 0)))
    live_float = live_row.astype(jnp.float32)
    padded_live = jnp.pad(live_float, (WIN, WIN))
    empty = jnp.zeros((FRAMES + 2 * WIN, INNER), jnp.float32)
    key_pos = jnp.arange(key_span, dtype=jnp.int32) - WIN
    query_pos = jnp.arange(block_rows, dtype=jnp.int32)
    in_window = jnp.abs(query_pos[:, None] - key_pos[None, :]) <= WIN

    def step(carry, index):
        key_grads, value_grads = carry
        first_row = (index * block_rows).astype(jnp.int32)
        query_blk = lax.dynamic_slice_in_dim(query, first_row, block_rows, 0)
        grad_blk = lax.dynamic_slice_in_dim(grad_att, first_row, block_rows, 0)
        query_live = lax.dynamic_slice_in_dim(live_float, first_row, block_rows, 0)
        key_blk = lax.dynamic_slice_in_dim(padded_keys, first_row, key_span, 0)
        value_blk = lax.dynamic_slice_in_dim(padded_values, first_row, key_span, 0)
        key_live = lax.dynamic_slice_in_dim(padded_live, first_row, key_span, 0)
        allowed = in_window & (key_live[None, :] > 0.5)
        attended, grad_query, grad_key, grad_value = block_terms(query_blk, key_blk, value_blk, grad_blk, allowed, query_live)
        key_grads = lax.dynamic_update_slice_in_dim(key_grads, lax.dynamic_slice_in_dim(key_grads, first_row, key_span, 0) + grad_key, first_row, 0)
        value_grads = lax.dynamic_update_slice_in_dim(value_grads, lax.dynamic_slice_in_dim(value_grads, first_row, key_span, 0) + grad_value, first_row, 0)
        return ((key_grads, value_grads), (attended, grad_query))
    (key_grads, value_grads), (attended, grad_query) = lax.scan(step, (empty, empty), jnp.arange(block_count, dtype=jnp.int32))
    return (attended.reshape(FRAMES, INNER), grad_query.reshape(FRAMES, INNER), key_grads[WIN:WIN + FRAMES], value_grads[WIN:WIN + FRAMES])

def reference(frames, live, norm_gain, w_qkv, w_out, cotangent):

    def one_sequence(inputs):
        frame_rows, live_row, upstream = inputs
        hidden = frame_rows.astype(jnp.float32)
        unit_rows, inverse = norm_rows(hidden)
        normed = (unit_rows * norm_gain).astype(jnp.bfloat16)
        projected = jnp.dot(normed, w_qkv, preferred_element_type=jnp.float32).astype(jnp.bfloat16)
        query = projected[:, :INNER]
        keys = projected[:, INNER:2 * INNER]
        values = projected[:, 2 * INNER:]
        live_float = live_row.astype(jnp.float32)
        grad_att = (jnp.dot(upstream, w_out.T, preferred_element_type=jnp.float32) * live_float[:, None]).astype(jnp.bfloat16)
        attended, grad_query, grad_key, grad_value = sequence_terms(query, keys, values, grad_att, live_row)
        grad_projected = jnp.concatenate([grad_query, grad_key, grad_value], axis=1).astype(jnp.bfloat16)
        term_qkv = jnp.dot(normed.T, grad_projected, preferred_element_type=jnp.float32)
        term_out = jnp.dot(attended.T, upstream, preferred_element_type=jnp.float32)
        grad_unit = jnp.dot(grad_projected, w_qkv.T, preferred_element_type=jnp.float32) * norm_gain
        through = inverse * (grad_unit - lax.optimization_barrier(jnp.mean(grad_unit, axis=-1, keepdims=True)) - unit_rows * lax.optimization_barrier(jnp.mean(grad_unit * unit_rows, axis=-1, keepdims=True)))
        grad_rows = (upstream.astype(jnp.float32) + through).astype(jnp.bfloat16)
        return (grad_rows, term_qkv, term_out)
    grad_rows, terms_qkv, terms_out = lax.map(one_sequence, (frames, live, cotangent))
    factor = 1.0 / math.sqrt(SEQS * FRAMES)
    return (grad_rows, lax.optimization_barrier(jnp.sum(terms_qkv, axis=0)) * factor, lax.optimization_barrier(jnp.sum(terms_out, axis=0)) * factor)
```

```python
import functools
import math

import jax
import jax.numpy as jnp
from jax import lax
from jax.experimental import pallas as pl
from jax.experimental.pallas import tpu as pltpu
from jax.sharding import Mesh, PartitionSpec as P

HEAD_DIM = 64
WIN = 512
EPS = 1e-05
NEG = -1e30

ZL, X, ZH, Y, C = 4, 4, 2, 4, 2
CHIPS_Z = ZL * ZH
BF = jnp.bfloat16
F32 = jnp.float32


def dot(left, right, cl, cr):
    return lax.dot_general(left, right, (((cl,), (cr,)), ((), ())), preferred_element_type=F32)


def swap_core(value):
    return lax.ppermute(value, "c", [(0, 1), (1, 0)])


def along_seq(value, step):
    count = ZH * Y
    pairs = [(i, i + step) for i in range(count) if 0 <= i + step < count]
    return lax.ppermute(value, ("zh", "y"), pairs)


def spread_z(value, step):
    pairs = []
    for y in range(Y):
        for half in range(ZH):
            z = y + ZL * half
            to = (z + step) % CHIPS_Z
            src = ((z % ZL) * ZH + z // ZL) * Y + y
            dst = ((to % ZL) * ZH + to // ZL) * Y + y
            pairs.append((src, dst))
    return lax.ppermute(value, ("zl", "zh", "y"), pairs)


def both(core, own, other, axis):
    first = jnp.where(core == 0, own, other)
    second = jnp.where(core == 0, other, own)
    return jnp.concatenate([first, second], axis=axis)


def norm_rows(values_in):
    average = jnp.mean(values_in, axis=-1, keepdims=True)
    centred = values_in - average
    inverse = lax.rsqrt(jnp.mean(centred * centred, axis=-1, keepdims=True) + EPS)
    return (centred * inverse, inverse)


def attention_kernel(q_ref, g_ref, own_ref, prev_ref, next_ref, bias_ref, live_ref,
                     att_ref, dq_ref, down_ref, dprev_ref, dnext_ref):
    rows = 256
    chunks_k, chunks_v = ([], [])
    for ref in (prev_ref, own_ref, next_ref):
        for half in range(2):
            cols = slice(half * rows, (half + 1) * rows)
            chunks_k.append(ref[0, :, cols])
            chunks_v.append(ref[1, :, cols])
    grads_k, grads_v = ([None] * 6, [None] * 6)
    scale = 1.0 / math.sqrt(HEAD_DIM)
    for block in range(2):
        cols = slice(block * rows, (block + 1) * rows)
        keys_t = jnp.concatenate(chunks_k[block:block + 5], axis=1)
        values_t = jnp.concatenate(chunks_v[block:block + 5], axis=1)
        query = (q_ref[:, cols].astype(F32) * scale).astype(BF)
        grad = g_ref[:, cols]
        scores = dot(keys_t.T, query, 1, 0) + bias_ref[block]
        peak = jnp.max(scores, axis=0, keepdims=True)
        exponent = jnp.exp(scores - peak)
        inverse = 1.0 / jnp.sum(exponent, axis=0, keepdims=True)
        probs = exponent * inverse
        probs_b = probs.astype(BF)
        attended = (dot(values_t, probs_b, 1, 0) * live_ref[:, cols]).astype(BF)
        att_ref[:, cols] = attended
        delta = jnp.sum(grad.astype(F32) * attended.astype(F32), axis=0, keepdims=True)
        grad_probs = dot(values_t.T, grad, 1, 0)
        grad_scores = (probs * (grad_probs - delta)).astype(BF)
        dq_ref[:, cols] = (dot(keys_t, grad_scores, 1, 0) * scale).astype(BF)
        grad_k = dot(query, grad_scores, 1, 1)
        grad_v = dot(grad, probs_b, 1, 1)
        for i in range(5):
            part = slice(i * rows, (i + 1) * rows)
            at = block + i
            grads_k[at] = grad_k[:, part] if grads_k[at] is None else grads_k[at] + grad_k[:, part]
            grads_v[at] = grad_v[:, part] if grads_v[at] is None else grads_v[at] + grad_v[:, part]
    for index, ref in enumerate((dprev_ref, down_ref, dnext_ref)):
        for half in range(2):
            cols = slice(half * rows, (half + 1) * rows)
            ref[0, :, cols] = grads_k[2 * index + half].astype(ref.dtype)
            ref[1, :, cols] = grads_v[2 * index + half].astype(ref.dtype)


def attention(query, grad, own, before, after, bias, live):
    inner, rows = query.shape
    heads = inner // HEAD_DIM
    one = pl.BlockSpec((HEAD_DIM, rows), lambda h: (h, 0))
    two = pl.BlockSpec((2, HEAD_DIM, rows), lambda h: (0, h, 0))
    pair = (2, inner, rows)
    return pl.pallas_call(
        attention_kernel,
        grid=(heads,),
        in_specs=[one, one, two, two, two,
                  pl.BlockSpec(bias.shape, lambda h: (0, 0, 0)),
                  pl.BlockSpec(live.shape, lambda h: (0, 0))],
        out_specs=[one, one, two, two, two],
        out_shape=[
            jax.ShapeDtypeStruct((inner, rows), BF),
            jax.ShapeDtypeStruct((inner, rows), BF),
            jax.ShapeDtypeStruct(pair, F32),
            jax.ShapeDtypeStruct(pair, BF),
            jax.ShapeDtypeStruct(pair, BF),
        ],
        name="attention",
    )(query, grad, own, before, after, bias, live)


def weight_kernel(rows_ref, grads_ref, out_ref):
    block = rows_ref.shape[2]
    left = rows_ref[...].reshape(ZL * block, rows_ref.shape[3])
    product = dot(left, grads_ref[...], 1, 1).astype(BF)
    for zl in range(ZL):
        for zh in range(ZH):
            for y in range(Y):
                lanes = (zh * Y + y) * 128
                out_ref[0, y, zl, zh] = product[zl * block:(zl + 1) * block, lanes:lanes + 128]


def weight_terms(rows_t, grads):
    block = rows_t.shape[0] // (ZL * X)
    count = rows_t.shape[1]
    return pl.pallas_call(
        weight_kernel,
        grid=(X,),
        in_specs=[
            pl.BlockSpec((ZL, 1, block, count), lambda x: (0, x, 0, 0)),
            pl.BlockSpec(grads.shape, lambda x: (0, 0)),
        ],
        out_specs=pl.BlockSpec((1, Y, ZL, ZH, block, 128), lambda x: (x, 0, 0, 0, 0, 0)),
        out_shape=jax.ShapeDtypeStruct((X, Y, ZL, ZH, block, 128), BF),
        name="weight_terms",
    )(rows_t.reshape(ZL, X, block, count), grads)


def to_owners_xy(blocks):
    flat = blocks.reshape((X * Y, ZL * ZH) + blocks.shape[4:])
    got = lax.all_to_all(flat, ("x", "y"), 0, 0, tiled=True)
    return jnp.sum(got.astype(F32), axis=0).astype(BF)


def body(frames, live, norm_gain, w_qkv, w_out, cotangent):
    core = lax.axis_index("c")
    is_home = lax.axis_index("zl") == lax.axis_index("y")
    length = frames.shape[1]
    model = frames.shape[2]
    half = w_qkv.shape[1] // 6
    shard = w_qkv.shape[0]
    shards = ZL * X

    mine = lax.dynamic_index_in_dim(w_qkv.reshape(shard, 3, 2, half), core, 2, keepdims=False)
    out_cols = lax.dynamic_index_in_dim(w_out.reshape(shard // 2, 2, 2 * half), core, 1, keepdims=False)
    out_cols = jnp.concatenate([out_cols[:, :half], out_cols[:, half:]], axis=0)
    payload = jnp.concatenate([mine[:, 1], mine[:, 2], mine[:, 0], out_cols], axis=1)
    moved = [spread_z(payload, step) for step in (1, -1, 2)]
    piece = jnp.where(is_home, payload, moved[0] + moved[1] + moved[2])

    def gather_xy(rows):
        spread = jnp.broadcast_to(rows[None], (shards,) + rows.shape)
        return lax.all_to_all(spread, ("y", "x"), 0, 0, tiled=True)

    upstream = cotangent[0]
    upstream_2 = both(core, upstream, swap_core(upstream), 0)
    live_own = live[0].astype(F32)[None]
    live_2 = both(core, live_own, swap_core(live_own), 1)
    live_before, live_after = along_seq(live_2, 1), along_seq(live_2, -1)
    hidden = frames[0].astype(F32)
    unit_rows, inverse = norm_rows(hidden)
    normed = (unit_rows * norm_gain).astype(BF)
    normed_2 = both(core, normed, swap_core(normed), 0)
    normed_t = normed_2.T

    span = length + 2 * WIN
    key_pos = jnp.arange(span, dtype=jnp.int32) - WIN
    query_pos = jnp.arange(length, dtype=jnp.int32)
    in_window = jnp.abs(query_pos[None, :] - key_pos[:, None]) <= WIN
    live_all = jnp.concatenate([live_before, live_2, live_after], axis=1)[0]
    bias = jnp.stack([
        jnp.where(in_window & (live_all[i * length:i * length + span, None] > 0.5), 0.0, NEG)
        for i in range(2)
    ])

    w_kv = gather_xy(piece[:, :2 * half]).reshape(model, 2 * half)
    pairs = dot(w_kv, normed_2, 0, 1).astype(BF)
    before, after = along_seq(pairs, 1), along_seq(pairs, -1)

    w_qo = gather_xy(piece[:, 2 * half:])
    w_q = w_qo[:, :, :half].reshape(model, half)
    out_part = w_qo[:, :, half:].reshape(shards, 2, shard // 2, half)
    out_part = out_part.transpose(0, 2, 1, 3).reshape(2, half, 2 * half)
    out_mine = lax.dynamic_index_in_dim(out_part, core, 0, keepdims=False)
    out_send = lax.dynamic_index_in_dim(out_part, 1 - core, 0, keepdims=False)
    w_o = both(core, out_mine, swap_core(out_send), 1)
    query = dot(w_q, normed_2, 0, 1).astype(BF)
    grad_att = (dot(w_o, upstream_2, 1, 1) * live_2).astype(BF)

    pair_shape = (2, half, 2 * length)
    attended, grad_query, grad_own, grad_before, grad_after = attention(
        query, grad_att, pairs.reshape(pair_shape), before.reshape(pair_shape),
        after.reshape(pair_shape), bias, live_2,
    )
    from_after = along_seq(grad_before, -1)
    from_before = along_seq(grad_after, 1)

    attended_all = both(core, attended, swap_core(attended), 0)
    blocks = ZH * Y
    cot_mine = lax.dynamic_index_in_dim(
        upstream_2.reshape(2 * length, blocks, 2, model // (2 * blocks)), core, 2, keepdims=False)
    cot_mine = jnp.pad(cot_mine, ((0, 0), (0, 0), (0, 128 - cot_mine.shape[2]))).reshape(2 * length, blocks * 128)
    term_out = dot(attended_all, cot_mine, 1, 0).astype(BF)
    term_out = term_out.reshape(ZL, X, -1, ZH, Y, 128).transpose(1, 4, 0, 3, 2, 5)
    sum_out = to_owners_xy(term_out)

    grad_pairs = (grad_own + from_after.astype(F32) + from_before.astype(F32)).astype(BF)
    grads = jnp.concatenate([grad_query[None], grad_pairs], axis=0)
    grads_other = swap_core(grads)
    grads_all = both(core, grads[:, None], grads_other[:, None], 1)
    grads_mine = lax.dynamic_index_in_dim(
        grads_all.reshape(blocks, 2, -1, 2 * length), core, 1, keepdims=False)
    grads_mine = jnp.pad(grads_mine, ((0, 0), (0, 128 - grads_mine.shape[1]), (0, 0)))
    term_qkv = weight_terms(normed_t, grads_mine.reshape(blocks * 128, 2 * length))

    part = dot(grad_pairs.reshape(2 * half, 2 * length), w_kv, 0, 1) + dot(grad_query, w_q, 0, 1)
    part = part.reshape(2, length, model)
    part_send = lax.dynamic_index_in_dim(part, 1 - core, 0, keepdims=False).astype(BF)
    part_mine = lax.dynamic_index_in_dim(part, core, 0, keepdims=False)
    grad_unit = (part_mine + swap_core(part_send).astype(F32)) * norm_gain

    sum_qkv = to_owners_xy(term_qkv)
    sums = jnp.concatenate([sum_qkv, sum_out], axis=1)
    sums = lax.all_to_all(sums, ("zl", "zh"), 0, 0, tiled=True)
    factor = 1.0 / math.sqrt(shards * blocks * 2 * length)
    total = jnp.sum(sums.astype(F32), axis=0) * factor

    through = inverse * (
        grad_unit
        - jnp.mean(grad_unit, axis=-1, keepdims=True)
        - unit_rows * jnp.mean(grad_unit * unit_rows, axis=-1, keepdims=True)
    )
    grad_rows = (upstream.astype(F32) + through).astype(BF)[None]
    cols = w_qkv.shape[1] // (2 * blocks)
    return (grad_rows, total[:shard, :cols], total[shard:, :model // (2 * blocks)])


def solution(mesh):
    split = Mesh(mesh.devices.reshape(ZL, X, ZH, Y, C), ("zl", "x", "zh", "y", "c"))
    dp, seq = ("zl", "x"), ("zh", "y", "c")
    return jax.shard_map(
        body,
        mesh=split,
        in_specs=(P(dp, seq, None), P(dp, seq), P(), P(dp, None), P(dp, None), P(dp, seq, None)),
        out_specs=(P(dp, seq, None), P(dp, seq), P(dp, seq)),
        check_vma=False,
    )
```

```python
import math

import jax
import jax.numpy as jnp
from jax import lax
from jax.experimental import pallas as pl
from jax.experimental.pallas import tpu as pltpu
from jax.sharding import Mesh, PartitionSpec as P

HEAD_DIM = 64
WIN = 512
EPS = 1e-05
NEG = -1e30

ZL, X, ZH, Y, C = 4, 4, 2, 4, 2
CHIPS_Z = ZL * ZH
BF = jnp.bfloat16
F32 = jnp.float32


def dot(left, right, cl, cr):
    return lax.dot_general(left, right, (((cl,), (cr,)), ((), ())), preferred_element_type=F32)


def swap_core(value):
    return lax.ppermute(value, "c", [(0, 1), (1, 0)])


def along_y(value, step):
    pairs = [(i, i + step) for i in range(Y) if 0 <= i + step < Y]
    return lax.ppermute(value, "y", pairs)


def across_y(value):
    return lax.ppermute(value, ("zh", "y"), [(Y - 1, 0), (Y, 2 * Y - 1)])


def across_z(value):
    return lax.ppermute(value, ("zh", "y"), [(0, Y), (2 * Y - 1, Y - 1)])


def across(value):
    return lax.ppermute(value, ("zh", "y"), [(Y - 1, Y), (Y, Y - 1)])


def spread_z(value, step):
    pairs = []
    for y in range(Y):
        for half in range(ZH):
            z = y + ZL * half
            to = (z + step) % CHIPS_Z
            src = ((z % ZL) * ZH + z // ZL) * Y + y
            dst = ((to % ZL) * ZH + to // ZL) * Y + y
            pairs.append((src, dst))
    return lax.ppermute(value, ("zl", "zh", "y"), pairs)


def both(core, own, other, axis):
    first = jnp.where(core == 0, own, other)
    second = jnp.where(core == 0, other, own)
    return jnp.concatenate([first, second], axis=axis)


def norm_rows(values_in):
    average = jnp.mean(values_in, axis=-1, keepdims=True)
    centred = values_in - average
    inverse = lax.rsqrt(jnp.mean(centred * centred, axis=-1, keepdims=True) + EPS)
    return (centred * inverse, inverse)


def attention_kernel(flag_ref, q_ref, g_ref, own_ref, prev_ref, next_ref, across_ref, bias_ref, live_ref,
                     att_ref, dq_ref, down_ref, dprev_ref, dnext_ref, dacross_ref):
    rows = 256
    last = flag_ref[1].astype(F32)
    first = flag_ref[2].astype(F32)
    chunks_k, chunks_v = ([], [])
    for ref, share in ((prev_ref, first), (own_ref, None), (next_ref, last)):
        for half in range(2):
            cols = slice(half * rows, (half + 1) * rows)
            for kind, chunks in ((0, chunks_k), (1, chunks_v)):
                chunk = ref[kind, :, cols]
                if share is not None:
                    chunk = (chunk.astype(F32) + across_ref[kind, :, cols].astype(F32) * share).astype(BF)
                chunks.append(chunk)
    grads_k, grads_v = ([None] * 6, [None] * 6)
    scale = 1.0 / math.sqrt(HEAD_DIM)
    for block in range(2):
        cols = slice(block * rows, (block + 1) * rows)
        keys_t = jnp.concatenate(chunks_k[block:block + 5], axis=1)
        values_t = jnp.concatenate(chunks_v[block:block + 5], axis=1)
        query = (q_ref[:, cols].astype(F32) * scale).astype(BF)
        grad = g_ref[:, cols]
        scores = dot(keys_t.T, query, 1, 0) + bias_ref[block]
        peak = jnp.max(scores, axis=0, keepdims=True)
        exponent = jnp.exp(scores - peak)
        inverse = 1.0 / jnp.sum(exponent, axis=0, keepdims=True)
        probs = exponent * inverse
        probs_b = probs.astype(BF)
        attended = (dot(values_t, probs_b, 1, 0) * live_ref[:, cols]).astype(BF)
        att_ref[:, cols] = attended
        delta = jnp.sum(grad.astype(F32) * attended.astype(F32), axis=0, keepdims=True)
        grad_probs = dot(values_t.T, grad, 1, 0)
        grad_scores = (probs * (grad_probs - delta)).astype(BF)
        dq_ref[:, cols] = (dot(keys_t, grad_scores, 1, 0) * scale).astype(BF)
        grad_k = dot(query, grad_scores, 1, 1)
        grad_v = dot(grad, probs_b, 1, 1)
        for i in range(5):
            part = slice(i * rows, (i + 1) * rows)
            at = block + i
            grads_k[at] = grad_k[:, part] if grads_k[at] is None else grads_k[at] + grad_k[:, part]
            grads_v[at] = grad_v[:, part] if grads_v[at] is None else grads_v[at] + grad_v[:, part]
    for kind, grads in ((0, grads_k), (1, grads_v)):
        for half in range(2):
            cols = slice(half * rows, (half + 1) * rows)
            dprev_ref[kind, :, cols] = grads[half].astype(BF)
            down_ref[kind, :, cols] = grads[2 + half]
            dnext_ref[kind, :, cols] = grads[4 + half].astype(BF)
            dacross_ref[kind, :, cols] = (grads[half] * first + grads[4 + half] * last).astype(BF)


SCALARS = pl.BlockSpec(memory_space=pltpu.SMEM)


def attention(flags, query, grad, own, before, after, beyond, bias, live):
    inner, rows = query.shape
    heads = inner // HEAD_DIM
    one = pl.BlockSpec((HEAD_DIM, rows), lambda h: (h, 0))
    two = pl.BlockSpec((2, HEAD_DIM, rows), lambda h: (0, h, 0))
    pair = (2, inner, rows)
    return pl.pallas_call(
        attention_kernel,
        grid=(heads,),
        in_specs=[SCALARS, one, one, two, two, two, two,
                  pl.BlockSpec(bias.shape, lambda h: (0, 0, 0)),
                  pl.BlockSpec(live.shape, lambda h: (0, 0))],
        out_specs=[one, one, two, two, two, two],
        out_shape=[
            jax.ShapeDtypeStruct((inner, rows), BF),
            jax.ShapeDtypeStruct((inner, rows), BF),
            jax.ShapeDtypeStruct(pair, F32),
            jax.ShapeDtypeStruct(pair, BF),
            jax.ShapeDtypeStruct(pair, BF),
            jax.ShapeDtypeStruct(pair, BF),
        ],
        name="attention",
    )(flags, query, grad, own, before, after, beyond, bias, live)


def turn_kernel(in_ref, out_ref):
    out_ref[...] = in_ref[...].T


def turn(value):
    rows, cols = value.shape
    step = 256
    return pl.pallas_call(
        turn_kernel,
        grid=(cols // step,),
        in_specs=[pl.BlockSpec((rows, step), lambda i: (0, i))],
        out_specs=pl.BlockSpec((step, rows), lambda i: (i, 0)),
        out_shape=jax.ShapeDtypeStruct((cols, rows), value.dtype),
        name="turn",
    )(value)


def out_grad_kernel(flag_ref, own_ref, other_ref, cot_ref, live_ref, out_ref):
    core = flag_ref[0]
    shards, rows, cols = own_ref.shape
    block = rows // 2
    total = None
    for ref, which in ((own_ref, core), (other_ref, 1 - core)):
        weights = ref[...].reshape(shards * rows, cols)
        cot = cot_ref[:, pl.ds(pl.multiple_of(which * 2 * cols, 128), 2 * cols)]
        for half in range(2):
            product = dot(weights, cot[:, half * cols:(half + 1) * cols], 1, 1)
            parts = [product[i * rows + half * block:i * rows + (half + 1) * block] for i in range(shards)]
            total = parts if total is None else [t + p for t, p in zip(total, parts)]
    out_ref[...] = (jnp.concatenate(total, axis=0) * live_ref[...]).astype(BF)


def out_grads(flags, own, other, cot, live):
    full = pl.BlockSpec(memory_space=pltpu.VMEM)
    return pl.pallas_call(
        out_grad_kernel,
        in_specs=[SCALARS, full, full, full, full],
        out_specs=full,
        out_shape=jax.ShapeDtypeStruct((own.shape[0] * own.shape[1] // 2, cot.shape[0]), BF),
        name="out_grads",
    )(flags, own, other, cot, live)


TAIL = 32


def out_kernel(flag_ref, own_ref, other_ref, cot_ref, out_ref, sum_ref):
    core = flag_ref[0]
    half = own_ref.shape[0]
    block = half // (ZL * X // 2)
    sum_ref[pl.ds(pl.multiple_of(core * half, 64), half)] = dot(own_ref[...], cot_ref[...], 1, 0)
    sum_ref[pl.ds(pl.multiple_of((1 - core) * half, 64), half)] = dot(other_ref[...], cot_ref[...], 1, 0)
    for x in range(X):
        for y in range(Y):
            tails = []
            for zl in range(ZL):
                rows = slice((zl * X + x) * block, (zl * X + x + 1) * block)
                out_ref[x, y, zl * block:(zl + 1) * block] = sum_ref[rows, y * 128:(y + 1) * 128]
                begin = Y * 128 + y * TAIL
                tails.append(sum_ref[rows, begin:begin + TAIL])
            out_ref[x, y, ZL * block:] = jnp.concatenate(tails, axis=1)


def out_terms(flags, own, other, cot):
    block = own.shape[0] // (ZL * X // 2)
    full = pl.BlockSpec(memory_space=pltpu.VMEM)
    return pl.pallas_call(
        out_kernel,
        in_specs=[SCALARS, full, full, full],
        out_specs=full,
        out_shape=jax.ShapeDtypeStruct((X, Y, (ZL + 1) * block, 128), F32),
        scratch_shapes=[pltpu.VMEM((2 * own.shape[0], cot.shape[1]), F32)],
        name="out_terms",
    )(flags, own, other, cot)


def weight_kernel(flag_ref, rows_ref, far_rows_ref, own_ref, other_ref, extra_ref, out_ref, near_ref, far_ref, sum_ref):
    block = rows_ref.shape[2]
    count = rows_ref.shape[3]
    half = own_ref.shape[1]
    cols = 3 * 2 * half // (ZH * Y * C)

    def assemble(core):
        for at in range(ZH * Y):
            near, far = ([], [])
            begin = (2 * at + core) * cols
            end = begin + cols
            while begin < end:
                kind, which, row = begin // (2 * half), begin // half % 2, begin % half
                size = min(end - begin, half - row)
                ref = own_ref if which == core else other_ref
                near.append(ref[kind].astype(F32)[row:row + size])
                if kind == 0:
                    far.append(jnp.zeros((size, count), F32))
                else:
                    far.append(ref[kind + 2].astype(F32)[row:row + size])
                begin += size
            pad = jnp.zeros((128 - cols, count), F32)
            near_ref[at * 128:(at + 1) * 128] = jnp.concatenate(near + [pad], axis=0).astype(BF)
            far_ref[at * 128:(at + 1) * 128] = jnp.concatenate(far + [pad], axis=0).astype(BF)

    start = pl.program_id(0) == 0

    @pl.when(start & (flag_ref[0] == 0))
    def _():
        assemble(0)

    @pl.when(start & (flag_ref[0] == 1))
    def _():
        assemble(1)

    sum_ref[...] = dot(rows_ref[...].reshape(ZL * block, count), near_ref[...], 1, 1)

    @pl.when(flag_ref[1] + flag_ref[2] > 0)
    def _():
        sum_ref[...] += dot(far_rows_ref[...].reshape(ZL * block, count), far_ref[...], 1, 1)

    for zl in range(ZL):
        for zh in range(ZH):
            for y in range(Y):
                lanes = (zh * Y + y) * 128
                at = (zl * ZH + zh) * block
                out_ref[0, y, at:at + block] = sum_ref[zl * block:(zl + 1) * block, lanes:lanes + 128].astype(BF)
    out_ref[0, :, ZL * ZH * block:] = extra_ref[0].astype(BF)


def weight_terms(flags, rows_t, far_rows_t, own, other, extra):
    block = rows_t.shape[0] // (ZL * X)
    count = rows_t.shape[1]
    left = pl.BlockSpec((ZL, 1, block, count), lambda x: (0, x, 0, 0))
    right = pl.BlockSpec(own.shape, lambda x: (0, 0, 0))
    lanes = ZH * Y * 128
    height = ZL * ZH * block + extra.shape[2]
    return pl.pallas_call(
        weight_kernel,
        grid=(X,),
        in_specs=[SCALARS, left, left, right, right,
                  pl.BlockSpec((1,) + extra.shape[1:], lambda x: (x, 0, 0, 0))],
        out_specs=pl.BlockSpec((1, Y, height, 128), lambda x: (x, 0, 0, 0)),
        out_shape=jax.ShapeDtypeStruct((X, Y, height, 128), BF),
        scratch_shapes=[
            pltpu.VMEM((lanes, count), BF),
            pltpu.VMEM((lanes, count), BF),
            pltpu.VMEM((ZL * block, lanes), F32),
        ],
        name="weight_terms",
    )(flags, rows_t.reshape(ZL, X, block, count), far_rows_t.reshape(ZL, X, block, count), own, other, extra)


def body(frames, live, norm_gain, w_qkv, w_out, cotangent):
    core = lax.axis_index("c")
    chip = lax.axis_index("zh") * Y + lax.axis_index("y")
    flags = jnp.stack([core, chip == Y - 1, chip == Y]).astype(jnp.int32)
    is_home = lax.axis_index("zl") == lax.axis_index("y")
    length = frames.shape[1]
    model = frames.shape[2]
    half = w_qkv.shape[1] // 6
    shard = w_qkv.shape[0]
    shards = ZL * X

    mine = lax.dynamic_index_in_dim(w_qkv.reshape(shard, 3, 2, half), core, 2, keepdims=False)
    out_cols = lax.dynamic_index_in_dim(w_out.reshape(shard // 2, 2, 2 * half), core, 1, keepdims=False)
    out_cols = jnp.concatenate([out_cols[:, :half], out_cols[:, half:]], axis=0)
    payload = jnp.concatenate([mine[:, 1], mine[:, 2], out_cols, mine[:, 0]], axis=1)
    moved = []
    for step in (1, -1, 2):
        moved.append(spread_z(payload, step))
    piece = jnp.where(is_home, payload, moved[0] + moved[1] + moved[2])

    live_own = live[0].astype(F32)[None]
    marks = jnp.pad(live_own.astype(BF), ((0, 15), (0, model - length)))
    far = across_y(jnp.concatenate([frames[0], marks], axis=0))
    far = across_z(far)
    live_2 = both(core, live_own, swap_core(live_own), 1)
    unit_rows, inverse = norm_rows(frames[0].astype(F32))
    normed = (unit_rows * norm_gain).astype(BF)
    upstream = cotangent[0]
    upstream_other = swap_core(upstream)
    upstream_2 = both(core, upstream, upstream_other, 0)
    normed_other = swap_core(normed)
    normed_2 = both(core, normed, normed_other, 0)
    normed_t = turn(normed_2)
    blocks = ZH * Y
    width = model // (2 * blocks)
    cot_mine = lax.dynamic_index_in_dim(
        upstream_2.reshape(2 * length, ZH, Y, 2, width), core, 3, keepdims=False)
    cot_mine = cot_mine.transpose(0, 2, 1, 3).reshape(2 * length, Y, ZH * width)
    cot_mine = jnp.concatenate([
        cot_mine[:, :, :128].reshape(2 * length, Y * 128),
        cot_mine[:, :, 128:].reshape(2 * length, Y * TAIL)], axis=1)

    spread = jnp.broadcast_to(piece[None], (shards,) + piece.shape)
    weights = lax.all_to_all(spread, ("y", "x"), 0, 0, tiled=True)
    w_kv = weights[:, :, :2 * half].reshape(model, 2 * half)
    pairs = dot(w_kv, normed_2, 0, 1).astype(BF)
    before = along_y(pairs, 1)
    after = along_y(pairs, -1)
    w_o = weights[:, :, 2 * half:3 * half]
    count = shards // 2
    w_o_mine = lax.dynamic_slice_in_dim(w_o, core * count, count, 0)
    w_o_other = swap_core(lax.dynamic_slice_in_dim(w_o, (1 - core) * count, count, 0))
    grad_att = out_grads(flags, w_o_mine, w_o_other, upstream_2, live_2)
    w_q = weights[:, :, 3 * half:].reshape(model, half)
    query = dot(w_q, normed_2, 0, 1).astype(BF)

    far, _ = lax.optimization_barrier((far, pairs))
    far_live = far[length:length + 1, :length].astype(F32)
    far_live = both(core, far_live, swap_core(far_live), 1)
    far = (norm_rows(far[:length].astype(F32))[0] * norm_gain).astype(BF)
    far_2 = both(core, far, swap_core(far), 0)
    beyond = dot(w_kv, far_2, 0, 1).astype(BF)

    live_before = along_y(live_2, 1) + far_live * flags[2].astype(F32)
    live_after = along_y(live_2, -1) + far_live * flags[1].astype(F32)
    span = length + 2 * WIN
    key_pos = jnp.arange(span, dtype=jnp.int32) - WIN
    query_pos = jnp.arange(length, dtype=jnp.int32)
    in_window = jnp.abs(query_pos[None, :] - key_pos[:, None]) <= WIN
    live_all = jnp.concatenate([live_before, live_2, live_after], axis=1)[0]
    bias = jnp.stack([
        jnp.where(in_window & (live_all[i * length:i * length + span, None] > 0.5), 0.0, NEG)
        for i in range(2)
    ])

    pair_shape = (2, half, 2 * length)
    attended, grad_query, grad_own, grad_before, grad_after, grad_far = attention(
        flags, query, grad_att, pairs.reshape(pair_shape), before.reshape(pair_shape),
        after.reshape(pair_shape), beyond.reshape(pair_shape), bias, live_2,
    )
    from_after = along_y(grad_before, -1)
    from_before = along_y(grad_after, 1)
    from_far = across(grad_far)

    attended_other = swap_core(attended)
    term_out = out_terms(flags, attended, attended_other, cot_mine)
    far_2, _ = lax.optimization_barrier((far_2, grad_own))
    far_t = turn(far_2)
    grad_own, term_out, far_t = lax.optimization_barrier((grad_own, term_out, far_t))

    grad_pairs = (grad_own + from_after.astype(F32) + from_before.astype(F32)).astype(BF)
    grads = jnp.concatenate([grad_query[None], grad_pairs, grad_far], axis=0)
    grads_other = swap_core(grads)
    terms = weight_terms(flags, normed_t, far_t, grads, grads_other, term_out)
    grad_pairs, terms = lax.optimization_barrier((grad_pairs, terms))
    got = lax.all_to_all(terms.reshape((X * Y,) + terms.shape[2:]), ("x", "y"), 0, 0, tiled=True)

    grad_pairs = (grad_pairs.astype(F32) + from_far.astype(F32)).astype(BF).reshape(2 * half, 2 * length)
    part = dot(grad_pairs, w_kv, 0, 1) + dot(grad_query, w_q, 0, 1)
    part = part.reshape(2, length, model)
    part_send = lax.dynamic_index_in_dim(part, 1 - core, 0, keepdims=False).astype(BF)
    part_mine = lax.dynamic_index_in_dim(part, core, 0, keepdims=False)
    grad_unit = (part_mine + swap_core(part_send).astype(F32)) * norm_gain

    sums = jnp.sum(got.astype(F32), axis=0).astype(BF)
    owners = ZL * ZH
    block = shard // 2
    sum_qkv = sums[:owners * shard].reshape(owners, shard, 128)
    sum_out = sums[owners * shard:]
    tails = sum_out[ZL * block:].reshape(block, ZL, TAIL).transpose(1, 0, 2)
    sum_out = jnp.concatenate([sum_out[:ZL * block].reshape(ZL, block, 128), tails], axis=2)
    sum_out = sum_out.reshape(ZL, block, ZH, width).transpose(0, 2, 1, 3).reshape(owners, block, width)
    sum_out = jnp.pad(sum_out, ((0, 0), (0, 0), (0, 128 - width)))
    sums = jnp.concatenate([sum_qkv, sum_out], axis=1)
    sums = lax.all_to_all(sums, ("zl", "zh"), 0, 0, tiled=True)
    factor = 1.0 / math.sqrt(shards * blocks * 2 * length)
    total = jnp.sum(sums.astype(F32), axis=0) * factor

    through = inverse * (
        grad_unit
        - jnp.mean(grad_unit, axis=-1, keepdims=True)
        - unit_rows * jnp.mean(grad_unit * unit_rows, axis=-1, keepdims=True)
    )
    grad_rows = (upstream.astype(F32) + through).astype(BF)[None]
    cols = w_qkv.shape[1] // (2 * blocks)
    return (grad_rows, total[:shard, :cols], total[shard:, :model // (2 * blocks)])


def solution(mesh):
    split = Mesh(mesh.devices.reshape(ZL, X, ZH, Y, C), ("zl", "x", "zh", "y", "c"))
    dp, seq = ("zl", "x"), ("zh", "y", "c")
    return jax.shard_map(
        body,
        mesh=split,
        in_specs=(P(dp, seq, None), P(dp, seq), P(), P(dp, None), P(dp, None), P(dp, seq, None)),
        out_specs=(P(dp, seq, None), P(dp, seq), P(dp, seq)),
        check_vma=False,
    )
```

```python
import math

import jax
import jax.numpy as jnp
from jax import lax
from jax.experimental import pallas as pl
from jax.experimental.pallas import tpu as pltpu
from jax.sharding import Mesh, PartitionSpec as P

HEAD_DIM = 64
WIN = 512
EPS = 1e-05
NEG = -1e30

ZL, X, ZH, Y, C = 4, 4, 2, 4, 2
CHIPS_Z = ZL * ZH
BF = jnp.bfloat16
F32 = jnp.float32


def dot(left, right, cl, cr):
    return lax.dot_general(left, right, (((cl,), (cr,)), ((), ())), preferred_element_type=F32)


def swap_core(value):
    return lax.ppermute(value, "c", [(0, 1), (1, 0)])


def along_y(value, step):
    pairs = [(i, i + step) for i in range(Y) if 0 <= i + step < Y]
    return lax.ppermute(value, "y", pairs)


def across(value):
    return lax.ppermute(value, ("zh", "y"), [(Y - 1, Y), (Y, Y - 1)])


def spread_z(value, step):
    pairs = []
    for y in range(Y):
        for half in range(ZH):
            z = y + ZL * half
            to = (z + step) % CHIPS_Z
            src = ((z % ZL) * ZH + z // ZL) * Y + y
            dst = ((to % ZL) * ZH + to // ZL) * Y + y
            pairs.append((src, dst))
    return lax.ppermute(value, ("zl", "zh", "y"), pairs)


def both(core, own, other, axis):
    first = jnp.where(core == 0, own, other)
    second = jnp.where(core == 0, other, own)
    return jnp.concatenate([first, second], axis=axis)


def norm_rows(values_in):
    average = jnp.mean(values_in, axis=-1, keepdims=True)
    centred = values_in - average
    inverse = lax.rsqrt(jnp.mean(centred * centred, axis=-1, keepdims=True) + EPS)
    return (centred * inverse, inverse)


def attention_kernel(flag_ref, q_ref, g_ref, own_ref, prev_ref, next_ref, across_ref, bias_ref, live_ref,
                     att_ref, dq_ref, down_ref, dprev_ref, dnext_ref, dacross_ref):
    rows = 256
    last = flag_ref[1].astype(F32)
    first = flag_ref[2].astype(F32)
    chunks_k, chunks_v = ([], [])
    for ref, share in ((prev_ref, first), (own_ref, None), (next_ref, last)):
        for half in range(2):
            cols = slice(half * rows, (half + 1) * rows)
            for kind, chunks in ((0, chunks_k), (1, chunks_v)):
                chunk = ref[kind, :, cols]
                if share is not None:
                    chunk = (chunk.astype(F32) + across_ref[kind, :, cols].astype(F32) * share).astype(BF)
                chunks.append(chunk)
    grads_k, grads_v = ([None] * 6, [None] * 6)
    scale = 1.0 / math.sqrt(HEAD_DIM)
    key_rows = jnp.concatenate(chunks_k, axis=1).T
    value_rows = jnp.concatenate(chunks_v, axis=1).T
    for block in range(2):
        span = slice(block * rows, (block + 5) * rows)
        cols = slice(block * rows, (block + 1) * rows)
        keys_t = jnp.concatenate(chunks_k[block:block + 5], axis=1)
        values_t = jnp.concatenate(chunks_v[block:block + 5], axis=1)
        query = (q_ref[:, cols].astype(F32) * scale).astype(BF)
        grad = g_ref[:, cols]
        scores = dot(key_rows[span], query, 1, 0) + bias_ref[block]
        peak = jnp.max(scores, axis=0, keepdims=True)
        exponent = jnp.exp(scores - peak)
        inverse = 1.0 / jnp.sum(exponent, axis=0, keepdims=True)
        probs = exponent * inverse
        probs_b = probs.astype(BF)
        attended = (dot(values_t, probs_b, 1, 0) * live_ref[:, cols]).astype(BF)
        att_ref[:, cols] = attended
        delta = jnp.sum(grad.astype(F32) * attended.astype(F32), axis=0, keepdims=True)
        grad_probs = dot(value_rows[span], grad, 1, 0)
        grad_scores = (probs * (grad_probs - delta)).astype(BF)
        dq_ref[:, cols] = (dot(keys_t, grad_scores, 1, 0) * scale).astype(BF)
        grad_k = dot(query, grad_scores, 1, 1)
        grad_v = dot(grad, probs_b, 1, 1)
        for i in range(5):
            part = slice(i * rows, (i + 1) * rows)
            at = block + i
            grads_k[at] = grad_k[:, part] if grads_k[at] is None else grads_k[at] + grad_k[:, part]
            grads_v[at] = grad_v[:, part] if grads_v[at] is None else grads_v[at] + grad_v[:, part]
    for kind, grads in ((0, grads_k), (1, grads_v)):
        for half in range(2):
            cols = slice(half * rows, (half + 1) * rows)
            dprev_ref[kind, :, cols] = grads[half].astype(BF)
            down_ref[kind, :, cols] = grads[2 + half]
            dnext_ref[kind, :, cols] = grads[4 + half].astype(BF)
            dacross_ref[kind, :, cols] = (grads[half] * first + grads[4 + half] * last).astype(BF)


SCALARS = pl.BlockSpec(memory_space=pltpu.SMEM)


def attention(flags, query, grad, own, before, after, beyond, bias, live):
    inner, rows = query.shape
    heads = inner // HEAD_DIM
    one = pl.BlockSpec((HEAD_DIM, rows), lambda h: (h, 0))
    two = pl.BlockSpec((2, HEAD_DIM, rows), lambda h: (0, h, 0))
    pair = (2, inner, rows)
    return pl.pallas_call(
        attention_kernel,
        grid=(heads,),
        in_specs=[SCALARS, one, one, two, two, two, two,
                  pl.BlockSpec(bias.shape, lambda h: (0, 0, 0)),
                  pl.BlockSpec(live.shape, lambda h: (0, 0))],
        out_specs=[one, one, two, two, two, two],
        out_shape=[
            jax.ShapeDtypeStruct((inner, rows), BF),
            jax.ShapeDtypeStruct((inner, rows), BF),
            jax.ShapeDtypeStruct(pair, F32),
            jax.ShapeDtypeStruct(pair, BF),
            jax.ShapeDtypeStruct(pair, BF),
            jax.ShapeDtypeStruct(pair, BF),
        ],
        name="attention",
    )(flags, query, grad, own, before, after, beyond, bias, live)


def turn_kernel(in_ref, out_ref):
    out_ref[...] = in_ref[...].T


def turn(value):
    rows, cols = value.shape
    step = 256
    return pl.pallas_call(
        turn_kernel,
        grid=(cols // step,),
        in_specs=[pl.BlockSpec((rows, step), lambda i: (0, i))],
        out_specs=pl.BlockSpec((step, rows), lambda i: (i, 0)),
        out_shape=jax.ShapeDtypeStruct((cols, rows), value.dtype),
        name="turn",
    )(value)


def out_grad_kernel(flag_ref, own_ref, other_ref, cot_ref, live_ref, out_ref):
    core = flag_ref[0]
    shards, rows, cols = own_ref.shape
    block = rows // 2
    total = None
    for ref, which in ((own_ref, core), (other_ref, 1 - core)):
        weights = ref[...].reshape(shards * rows, cols)
        cot = cot_ref[:, pl.ds(pl.multiple_of(which * 2 * cols, 128), 2 * cols)]
        for half in range(2):
            product = dot(weights, cot[:, half * cols:(half + 1) * cols], 1, 1)
            parts = [product[i * rows + half * block:i * rows + (half + 1) * block] for i in range(shards)]
            total = parts if total is None else [t + p for t, p in zip(total, parts)]
    out_ref[...] = (jnp.concatenate(total, axis=0) * live_ref[...]).astype(BF)


def out_grads(flags, own, other, cot, live):
    full = pl.BlockSpec(memory_space=pltpu.VMEM)
    return pl.pallas_call(
        out_grad_kernel,
        in_specs=[SCALARS, full, full, full, full],
        out_specs=full,
        out_shape=jax.ShapeDtypeStruct((own.shape[0] * own.shape[1] // 2, cot.shape[0]), BF),
        name="out_grads",
    )(flags, own, other, cot, live)


TAIL = 32


def out_kernel(flag_ref, own_ref, other_ref, cot_ref, out_ref, sum_ref):
    core = flag_ref[0]
    half = own_ref.shape[0]
    block = half // (ZL * X // 2)
    sum_ref[pl.ds(pl.multiple_of(core * half, 64), half)] = dot(own_ref[...], cot_ref[...], 1, 0)
    sum_ref[pl.ds(pl.multiple_of((1 - core) * half, 64), half)] = dot(other_ref[...], cot_ref[...], 1, 0)
    for x in range(X):
        for y in range(Y):
            tails = []
            for zl in range(ZL):
                rows = slice((zl * X + x) * block, (zl * X + x + 1) * block)
                out_ref[x, y, zl * block:(zl + 1) * block] = sum_ref[rows, y * 128:(y + 1) * 128]
                begin = Y * 128 + y * TAIL
                tails.append(sum_ref[rows, begin:begin + TAIL])
            out_ref[x, y, ZL * block:] = jnp.concatenate(tails, axis=1)


def out_terms(flags, own, other, cot):
    block = own.shape[0] // (ZL * X // 2)
    full = pl.BlockSpec(memory_space=pltpu.VMEM)
    return pl.pallas_call(
        out_kernel,
        in_specs=[SCALARS, full, full, full],
        out_specs=full,
        out_shape=jax.ShapeDtypeStruct((X, Y, (ZL + 1) * block, 128), F32),
        scratch_shapes=[pltpu.VMEM((2 * own.shape[0], cot.shape[1]), F32)],
        name="out_terms",
    )(flags, own, other, cot)


def weight_kernel(flag_ref, rows_ref, far_rows_ref, own_q, other_q, own_kv, other_kv, own_far, other_far,
                  extra_ref, out_ref, near_ref, far_ref, sum_ref):
    block = rows_ref.shape[2]
    count = rows_ref.shape[3]
    half = own_q.shape[0]
    cols = 3 * 2 * half // (ZH * Y * C)

    def assemble(core):
        for at in range(ZH * Y):
            near, far = ([], [])
            begin = (2 * at + core) * cols
            end = begin + cols
            while begin < end:
                kind, which, row = begin // (2 * half), begin // half % 2, begin % half
                size = min(end - begin, half - row)
                here = which == core
                if kind == 0:
                    near.append((own_q if here else other_q)[...].astype(F32)[row:row + size])
                    far.append(jnp.zeros((size, count), F32))
                else:
                    near.append((own_kv if here else other_kv)[kind - 1].astype(F32)[row:row + size])
                    far.append((own_far if here else other_far)[kind - 1].astype(F32)[row:row + size])
                begin += size
            pad = jnp.zeros((128 - cols, count), F32)
            near_ref[at * 128:(at + 1) * 128] = jnp.concatenate(near + [pad], axis=0).astype(BF)
            far_ref[at * 128:(at + 1) * 128] = jnp.concatenate(far + [pad], axis=0).astype(BF)

    start = pl.program_id(0) == 0

    @pl.when(start & (flag_ref[0] == 0))
    def _():
        assemble(0)

    @pl.when(start & (flag_ref[0] == 1))
    def _():
        assemble(1)

    sum_ref[...] = dot(rows_ref[...].reshape(ZL * block, count), near_ref[...], 1, 1)

    @pl.when(flag_ref[1] + flag_ref[2] > 0)
    def _():
        sum_ref[...] += dot(far_rows_ref[...].reshape(ZL * block, count), far_ref[...], 1, 1)

    for zl in range(ZL):
        for zh in range(ZH):
            for y in range(Y):
                lanes = (zh * Y + y) * 128
                at = (zl * ZH + zh) * block
                out_ref[0, y, at:at + block] = sum_ref[zl * block:(zl + 1) * block, lanes:lanes + 128].astype(BF)
    out_ref[0, :, ZL * ZH * block:] = extra_ref[0].astype(BF)


def weight_terms(flags, rows_t, far_rows_t, queries, pairs, far, extra):
    block = rows_t.shape[0] // (ZL * X)
    count = rows_t.shape[1]
    left = pl.BlockSpec((ZL, 1, block, count), lambda x: (0, x, 0, 0))
    one = pl.BlockSpec(queries[0].shape, lambda x: (0, 0))
    two = pl.BlockSpec(pairs[0].shape, lambda x: (0, 0, 0))
    lanes = ZH * Y * 128
    height = ZL * ZH * block + extra.shape[2]
    return pl.pallas_call(
        weight_kernel,
        grid=(X,),
        in_specs=[SCALARS, left, left, one, one, two, two, two, two,
                  pl.BlockSpec((1,) + extra.shape[1:], lambda x: (x, 0, 0, 0))],
        out_specs=pl.BlockSpec((1, Y, height, 128), lambda x: (x, 0, 0, 0)),
        out_shape=jax.ShapeDtypeStruct((X, Y, height, 128), BF),
        scratch_shapes=[
            pltpu.VMEM((lanes, count), BF),
            pltpu.VMEM((lanes, count), BF),
            pltpu.VMEM((ZL * block, lanes), F32),
        ],
        name="weight_terms",
    )(flags, rows_t.reshape(ZL, X, block, count), far_rows_t.reshape(ZL, X, block, count),
      *queries, *pairs, *far, extra)


def body(frames, live, norm_gain, w_qkv, w_out, cotangent):
    core = lax.axis_index("c")
    chip = lax.axis_index("zh") * Y + lax.axis_index("y")
    flags = jnp.stack([core, chip == Y - 1, chip == Y]).astype(jnp.int32)
    is_home = lax.axis_index("zl") == lax.axis_index("y")
    length = frames.shape[1]
    model = frames.shape[2]
    half = w_qkv.shape[1] // 6
    shard = w_qkv.shape[0]
    shards = ZL * X

    mine = lax.dynamic_index_in_dim(w_qkv.reshape(shard, 3, 2, half), core, 2, keepdims=False)
    out_cols = lax.dynamic_index_in_dim(w_out.reshape(shard // 2, 2, 2 * half), core, 1, keepdims=False)
    out_cols = jnp.concatenate([out_cols[:, :half], out_cols[:, half:]], axis=0)
    payload = jnp.concatenate([mine[:, 1], mine[:, 2], out_cols, mine[:, 0]], axis=1)
    moved = []
    for step in (1, -1, 2):
        moved.append(spread_z(payload, step))
    piece = jnp.where(is_home, payload, moved[0] + moved[1] + moved[2])

    live_own = live[0].astype(F32)[None]
    marks = jnp.pad(live_own.astype(BF), ((0, 15), (0, model - length)))
    far = across(jnp.concatenate([frames[0], marks], axis=0))
    live_2 = both(core, live_own, swap_core(live_own), 1)
    unit_rows, inverse = norm_rows(frames[0].astype(F32))
    normed = (unit_rows * norm_gain).astype(BF)
    upstream = cotangent[0]
    upstream_other = swap_core(upstream)
    upstream_2 = both(core, upstream, upstream_other, 0)
    normed_other = swap_core(normed)
    normed_2 = both(core, normed, normed_other, 0)
    normed_t = turn(normed_2)
    blocks = ZH * Y
    width = model // (2 * blocks)
    cot_mine = lax.dynamic_index_in_dim(
        upstream_2.reshape(2 * length, ZH, Y, 2, width), core, 3, keepdims=False)
    cot_mine = cot_mine.transpose(0, 2, 1, 3).reshape(2 * length, Y, ZH * width)
    cot_mine = jnp.concatenate([
        cot_mine[:, :, :128].reshape(2 * length, Y * 128),
        cot_mine[:, :, 128:].reshape(2 * length, Y * TAIL)], axis=1)

    spread = jnp.broadcast_to(piece[None], (shards,) + piece.shape)
    weights = lax.all_to_all(spread, ("y", "x"), 0, 0, tiled=True)
    w_kv = weights[:, :, :2 * half].reshape(model, 2 * half)
    pairs = dot(w_kv, normed_2, 0, 1).astype(BF)
    before = along_y(pairs, 1)
    after = along_y(pairs, -1)
    w_o = weights[:, :, 2 * half:3 * half]
    count = shards // 2
    w_o_mine = lax.dynamic_slice_in_dim(w_o, core * count, count, 0)
    w_o_other = swap_core(lax.dynamic_slice_in_dim(w_o, (1 - core) * count, count, 0))
    grad_att = out_grads(flags, w_o_mine, w_o_other, upstream_2, live_2)
    w_q = weights[:, :, 3 * half:].reshape(model, half)
    query = dot(w_q, normed_2, 0, 1).astype(BF)

    far, _ = lax.optimization_barrier((far, pairs))
    far_live = far[length:length + 1, :length].astype(F32)
    far_live = both(core, far_live, swap_core(far_live), 1)
    far = (norm_rows(far[:length].astype(F32))[0] * norm_gain).astype(BF)
    far_2 = both(core, far, swap_core(far), 0)
    beyond = dot(w_kv, far_2, 0, 1).astype(BF)

    live_before = along_y(live_2, 1) + far_live * flags[2].astype(F32)
    live_after = along_y(live_2, -1) + far_live * flags[1].astype(F32)
    span = length + 2 * WIN
    key_pos = jnp.arange(span, dtype=jnp.int32) - WIN
    query_pos = jnp.arange(length, dtype=jnp.int32)
    in_window = jnp.abs(query_pos[None, :] - key_pos[:, None]) <= WIN
    live_all = jnp.concatenate([live_before, live_2, live_after], axis=1)[0]
    bias = jnp.stack([
        jnp.where(in_window & (live_all[i * length:i * length + span, None] > 0.5), 0.0, NEG)
        for i in range(2)
    ])

    pair_shape = (2, half, 2 * length)
    attended, grad_query, grad_own, grad_before, grad_after, grad_far = attention(
        flags, query, grad_att, pairs.reshape(pair_shape), before.reshape(pair_shape),
        after.reshape(pair_shape), beyond.reshape(pair_shape), bias, live_2,
    )
    from_after = along_y(grad_before, -1)
    from_before = along_y(grad_after, 1)
    from_far = across(grad_far)

    attended_other = swap_core(attended)
    grad_query_other = swap_core(grad_query)
    grad_far_other = swap_core(grad_far)
    term_out = out_terms(flags, attended, attended_other, cot_mine)
    far_2, _ = lax.optimization_barrier((far_2, grad_own))
    far_t = turn(far_2)
    grad_own, term_out, far_t = lax.optimization_barrier((grad_own, term_out, far_t))

    grad_pairs = (grad_own + from_after.astype(F32) + from_before.astype(F32)).astype(BF)
    pairs_other = swap_core(grad_pairs)
    terms = weight_terms(flags, normed_t, far_t, (grad_query, grad_query_other), (grad_pairs, pairs_other),
                         (grad_far, grad_far_other), term_out)
    grad_pairs, terms = lax.optimization_barrier((grad_pairs, terms))
    got = lax.all_to_all(terms.reshape((X * Y,) + terms.shape[2:]), ("x", "y"), 0, 0, tiled=True)

    grad_pairs = (grad_pairs.astype(F32) + from_far.astype(F32)).astype(BF).reshape(2 * half, 2 * length)
    part = dot(grad_pairs, w_kv, 0, 1) + dot(grad_query, w_q, 0, 1)
    part = part.reshape(2, length, model)
    part_send = lax.dynamic_index_in_dim(part, 1 - core, 0, keepdims=False).astype(BF)
    part_mine = lax.dynamic_index_in_dim(part, core, 0, keepdims=False)
    grad_unit = (part_mine + swap_core(part_send).astype(F32)) * norm_gain

    sums = jnp.sum(got.astype(F32), axis=0).astype(BF)
    owners = ZL * ZH
    block = shard // 2
    sum_qkv = sums[:owners * shard].reshape(owners, shard, 128)
    sum_out = sums[owners * shard:]
    tails = sum_out[ZL * block:].reshape(block, ZL, TAIL).transpose(1, 0, 2)
    sum_out = jnp.concatenate([sum_out[:ZL * block].reshape(ZL, block, 128), tails], axis=2)
    sum_out = sum_out.reshape(ZL, block, ZH, width).transpose(0, 2, 1, 3).reshape(owners, block, width)
    sum_out = jnp.pad(sum_out, ((0, 0), (0, 0), (0, 128 - width)))
    sums = jnp.concatenate([sum_qkv, sum_out], axis=1)
    sums = lax.all_to_all(sums, ("zl", "zh"), 0, 0, tiled=True)
    factor = 1.0 / math.sqrt(shards * blocks * 2 * length)
    total = jnp.sum(sums.astype(F32), axis=0) * factor

    through = inverse * (
        grad_unit
        - jnp.mean(grad_unit, axis=-1, keepdims=True)
        - unit_rows * jnp.mean(grad_unit * unit_rows, axis=-1, keepdims=True)
    )
    grad_rows = (upstream.astype(F32) + through).astype(BF)[None]
    cols = w_qkv.shape[1] // (2 * blocks)
    return (grad_rows, total[:shard, :cols], total[shard:, :model // (2 * blocks)])


def solution(mesh):
    split = Mesh(mesh.devices.reshape(ZL, X, ZH, Y, C), ("zl", "x", "zh", "y", "c"))
    dp, seq = ("zl", "x"), ("zh", "y", "c")
    return jax.shard_map(
        body,
        mesh=split,
        in_specs=(P(dp, seq, None), P(dp, seq), P(), P(dp, None), P(dp, None), P(dp, seq, None)),
        out_specs=(P(dp, seq, None), P(dp, seq), P(dp, seq)),
        check_vma=False,
    )
```

```python
import math

import jax
import jax.numpy as jnp
from jax import lax
from jax.experimental import pallas as pl
from jax.experimental.pallas import tpu as pltpu
from jax.sharding import Mesh, PartitionSpec as P

HEAD_DIM = 64
WIN = 512
EPS = 1e-05
NEG = -1e30

ZL, X, ZH, Y, C = 4, 4, 2, 4, 2
CHIPS_Z = ZL * ZH
BF = jnp.bfloat16
F32 = jnp.float32


def dot(left, right, cl, cr):
    return lax.dot_general(left, right, (((cl,), (cr,)), ((), ())), preferred_element_type=F32)


def swap_core(value):
    return lax.ppermute(value, "c", [(0, 1), (1, 0)])


def along_y(value, step):
    pairs = [(i, i + step) for i in range(Y) if 0 <= i + step < Y]
    return lax.ppermute(value, "y", pairs)


def across(value):
    return lax.ppermute(value, ("zh", "y"), [(Y - 1, Y), (Y, Y - 1)])


def spread_z(value, step):
    pairs = []
    for y in range(Y):
        for half in range(ZH):
            z = y + ZL * half
            to = (z + step) % CHIPS_Z
            src = ((z % ZL) * ZH + z // ZL) * Y + y
            dst = ((to % ZL) * ZH + to // ZL) * Y + y
            pairs.append((src, dst))
    return lax.ppermute(value, ("zl", "zh", "y"), pairs)


def both(core, own, other, axis):
    first = jnp.where(core == 0, own, other)
    second = jnp.where(core == 0, other, own)
    return jnp.concatenate([first, second], axis=axis)


def norm_rows(values_in):
    average = jnp.mean(values_in, axis=-1, keepdims=True)
    centred = values_in - average
    inverse = lax.rsqrt(jnp.mean(centred * centred, axis=-1, keepdims=True) + EPS)
    return (centred * inverse, inverse)


def attention_kernel(flag_ref, q_ref, g_ref, own_ref, prev_ref, next_ref, across_ref, bias_ref, live_ref,
                     att_ref, dq_ref, down_ref, dprev_ref, dnext_ref, dacross_ref):
    rows = 256
    last = flag_ref[1].astype(F32)
    first = flag_ref[2].astype(F32)
    chunks_k, chunks_v = ([], [])
    for ref, share in ((prev_ref, first), (own_ref, None), (next_ref, last)):
        for half in range(2):
            cols = slice(half * rows, (half + 1) * rows)
            for kind, chunks in ((0, chunks_k), (1, chunks_v)):
                chunk = ref[kind, :, cols]
                if share is not None:
                    chunk = (chunk.astype(F32) + across_ref[kind, :, cols].astype(F32) * share).astype(BF)
                chunks.append(chunk)
    grads_k, grads_v = ([None] * 6, [None] * 6)
    scale = 1.0 / math.sqrt(HEAD_DIM)
    key_rows = jnp.concatenate(chunks_k, axis=1).T
    value_rows = jnp.concatenate(chunks_v, axis=1).T
    for block in range(2):
        span = slice(block * rows, (block + 5) * rows)
        cols = slice(block * rows, (block + 1) * rows)
        keys_t = jnp.concatenate(chunks_k[block:block + 5], axis=1)
        values_t = jnp.concatenate(chunks_v[block:block + 5], axis=1)
        query = (q_ref[:, cols].astype(F32) * scale).astype(BF)
        grad = g_ref[:, cols]
        scores = dot(key_rows[span], query, 1, 0) + bias_ref[block]
        peak = jnp.max(scores, axis=0, keepdims=True)
        exponent = jnp.exp(scores - peak)
        inverse = 1.0 / jnp.sum(exponent, axis=0, keepdims=True)
        probs = exponent * inverse
        probs_b = probs.astype(BF)
        attended = (dot(values_t, probs_b, 1, 0) * live_ref[:, cols]).astype(BF)
        att_ref[:, cols] = attended
        delta = jnp.sum(grad.astype(F32) * attended.astype(F32), axis=0, keepdims=True)
        grad_probs = dot(value_rows[span], grad, 1, 0)
        grad_scores = (probs * (grad_probs - delta)).astype(BF)
        dq_ref[:, cols] = (dot(keys_t, grad_scores, 1, 0) * scale).astype(BF)
        grad_k = dot(query, grad_scores, 1, 1)
        grad_v = dot(grad, probs_b, 1, 1)
        for i in range(5):
            part = slice(i * rows, (i + 1) * rows)
            at = block + i
            grads_k[at] = grad_k[:, part] if grads_k[at] is None else grads_k[at] + grad_k[:, part]
            grads_v[at] = grad_v[:, part] if grads_v[at] is None else grads_v[at] + grad_v[:, part]
    for kind, grads in ((0, grads_k), (1, grads_v)):
        for half in range(2):
            cols = slice(half * rows, (half + 1) * rows)
            dprev_ref[kind, :, cols] = grads[half].astype(BF)
            down_ref[kind, :, cols] = grads[2 + half]
            dnext_ref[kind, :, cols] = grads[4 + half].astype(BF)
            dacross_ref[kind, :, cols] = (grads[half] * first + grads[4 + half] * last).astype(BF)


SCALARS = pl.BlockSpec(memory_space=pltpu.SMEM)


def attention(flags, query, grad, own, before, after, beyond, bias, live):
    inner, rows = query.shape
    heads = inner // HEAD_DIM
    one = pl.BlockSpec((HEAD_DIM, rows), lambda h: (h, 0))
    two = pl.BlockSpec((2, HEAD_DIM, rows), lambda h: (0, h, 0))
    pair = (2, inner, rows)
    return pl.pallas_call(
        attention_kernel,
        grid=(heads,),
        in_specs=[SCALARS, one, one, two, two, two, two,
                  pl.BlockSpec(bias.shape, lambda h: (0, 0, 0)),
                  pl.BlockSpec(live.shape, lambda h: (0, 0))],
        out_specs=[one, one, two, two, two, two],
        out_shape=[
            jax.ShapeDtypeStruct((inner, rows), BF),
            jax.ShapeDtypeStruct((inner, rows), BF),
            jax.ShapeDtypeStruct(pair, F32),
            jax.ShapeDtypeStruct(pair, BF),
            jax.ShapeDtypeStruct(pair, BF),
            jax.ShapeDtypeStruct(pair, BF),
        ],
        name="attention",
    )(flags, query, grad, own, before, after, beyond, bias, live)


def turn_kernel(in_ref, out_ref):
    out_ref[...] = in_ref[...].T


def turn(value):
    rows, cols = value.shape
    step = 256
    return pl.pallas_call(
        turn_kernel,
        grid=(cols // step,),
        in_specs=[pl.BlockSpec((rows, step), lambda i: (0, i))],
        out_specs=pl.BlockSpec((step, rows), lambda i: (i, 0)),
        out_shape=jax.ShapeDtypeStruct((cols, rows), value.dtype),
        name="turn",
    )(value)


def out_grad_kernel(flag_ref, own_ref, other_ref, cot_ref, live_ref, out_ref):
    core = flag_ref[0]
    shards, rows, cols = own_ref.shape
    block = rows // 2
    total = None
    for ref, which in ((own_ref, core), (other_ref, 1 - core)):
        weights = ref[...].reshape(shards * rows, cols)
        cot = cot_ref[:, pl.ds(pl.multiple_of(which * 2 * cols, 128), 2 * cols)]
        for half in range(2):
            product = dot(weights, cot[:, half * cols:(half + 1) * cols], 1, 1)
            parts = [product[i * rows + half * block:i * rows + (half + 1) * block] for i in range(shards)]
            total = parts if total is None else [t + p for t, p in zip(total, parts)]
    out_ref[...] = (jnp.concatenate(total, axis=0) * live_ref[...]).astype(BF)


def out_grads(flags, own, other, cot, live):
    full = pl.BlockSpec(memory_space=pltpu.VMEM)
    return pl.pallas_call(
        out_grad_kernel,
        in_specs=[SCALARS, full, full, full, full],
        out_specs=full,
        out_shape=jax.ShapeDtypeStruct((own.shape[0] * own.shape[1] // 2, cot.shape[0]), BF),
        name="out_grads",
    )(flags, own, other, cot, live)


TAIL = 32


def out_kernel(flag_ref, own_ref, other_ref, cot_ref, out_ref, sum_ref):
    core = flag_ref[0]
    half = own_ref.shape[0]
    block = half // (ZL * X // 2)
    sum_ref[pl.ds(pl.multiple_of(core * half, 64), half)] = dot(own_ref[...], cot_ref[...], 1, 0)
    sum_ref[pl.ds(pl.multiple_of((1 - core) * half, 64), half)] = dot(other_ref[...], cot_ref[...], 1, 0)
    for x in range(X):
        for y in range(Y):
            tails = []
            for zl in range(ZL):
                rows = slice((zl * X + x) * block, (zl * X + x + 1) * block)
                out_ref[x, y, zl * block:(zl + 1) * block] = sum_ref[rows, y * 128:(y + 1) * 128]
                begin = Y * 128 + y * TAIL
                tails.append(sum_ref[rows, begin:begin + TAIL])
            out_ref[x, y, ZL * block:] = jnp.concatenate(tails, axis=1)


def out_terms(flags, own, other, cot):
    block = own.shape[0] // (ZL * X // 2)
    full = pl.BlockSpec(memory_space=pltpu.VMEM)
    return pl.pallas_call(
        out_kernel,
        in_specs=[SCALARS, full, full, full],
        out_specs=full,
        out_shape=jax.ShapeDtypeStruct((X, Y, (ZL + 1) * block, 128), F32),
        scratch_shapes=[pltpu.VMEM((2 * own.shape[0], cot.shape[1]), F32)],
        name="out_terms",
    )(flags, own, other, cot)


def weight_kernel(flag_ref, rows_ref, far_rows_ref, own_q, other_q, own_kv, other_kv, own_far, other_far,
                  extra_ref, out_ref, near_ref, far_ref, sum_ref):
    block = rows_ref.shape[2]
    count = rows_ref.shape[3]
    half = own_q.shape[0]
    cols = 3 * 2 * half // (ZH * Y * C)

    def assemble(core):
        for at in range(ZH * Y):
            near, far = ([], [])
            begin = (2 * at + core) * cols
            end = begin + cols
            while begin < end:
                kind, which, row = begin // (2 * half), begin // half % 2, begin % half
                size = min(end - begin, half - row)
                here = which == core
                if kind == 0:
                    near.append((own_q if here else other_q)[...].astype(F32)[row:row + size])
                    far.append(jnp.zeros((size, count), F32))
                else:
                    near.append((own_kv if here else other_kv)[kind - 1].astype(F32)[row:row + size])
                    far.append((own_far if here else other_far)[kind - 1].astype(F32)[row:row + size])
                begin += size
            pad = jnp.zeros((128 - cols, count), F32)
            near_ref[at * 128:(at + 1) * 128] = jnp.concatenate(near + [pad], axis=0).astype(BF)
            far_ref[at * 128:(at + 1) * 128] = jnp.concatenate(far + [pad], axis=0).astype(BF)

    start = pl.program_id(0) == 0

    @pl.when(start & (flag_ref[0] == 0))
    def _():
        assemble(0)

    @pl.when(start & (flag_ref[0] == 1))
    def _():
        assemble(1)

    sum_ref[...] = dot(rows_ref[...].reshape(ZL * block, count), near_ref[...], 1, 1)

    @pl.when(flag_ref[1] + flag_ref[2] > 0)
    def _():
        sum_ref[...] += dot(far_rows_ref[...].reshape(ZL * block, count), far_ref[...], 1, 1)

    for zl in range(ZL):
        for zh in range(ZH):
            for y in range(Y):
                lanes = (zh * Y + y) * 128
                at = (zl * ZH + zh) * block
                out_ref[0, y, at:at + block] = sum_ref[zl * block:(zl + 1) * block, lanes:lanes + 128].astype(BF)
    out_ref[0, :, ZL * ZH * block:] = extra_ref[0].astype(BF)


def weight_terms(flags, rows_t, far_rows_t, queries, pairs, far, extra):
    block = rows_t.shape[0] // (ZL * X)
    count = rows_t.shape[1]
    left = pl.BlockSpec((ZL, 1, block, count), lambda x: (0, x, 0, 0))
    one = pl.BlockSpec(queries[0].shape, lambda x: (0, 0))
    two = pl.BlockSpec(pairs[0].shape, lambda x: (0, 0, 0))
    lanes = ZH * Y * 128
    height = ZL * ZH * block + extra.shape[2]
    return pl.pallas_call(
        weight_kernel,
        grid=(X,),
        in_specs=[SCALARS, left, left, one, one, two, two, two, two,
                  pl.BlockSpec((1,) + extra.shape[1:], lambda x: (x, 0, 0, 0))],
        out_specs=pl.BlockSpec((1, Y, height, 128), lambda x: (x, 0, 0, 0)),
        out_shape=jax.ShapeDtypeStruct((X, Y, height, 128), BF),
        scratch_shapes=[
            pltpu.VMEM((lanes, count), BF),
            pltpu.VMEM((lanes, count), BF),
            pltpu.VMEM((ZL * block, lanes), F32),
        ],
        name="weight_terms",
    )(flags, rows_t.reshape(ZL, X, block, count), far_rows_t.reshape(ZL, X, block, count),
      *queries, *pairs, *far, extra)


def body(frames, live, norm_gain, w_qkv, w_out, cotangent):
    core = lax.axis_index("c")
    chip = lax.axis_index("zh") * Y + lax.axis_index("y")
    flags = jnp.stack([core, chip == Y - 1, chip == Y]).astype(jnp.int32)
    is_home = lax.axis_index("zl") == lax.axis_index("y")
    length = frames.shape[1]
    model = frames.shape[2]
    half = w_qkv.shape[1] // 6
    shard = w_qkv.shape[0]
    shards = ZL * X

    def chosen(array, at, size):
        return jnp.where(core == 0, array[:, at:at + size], array[:, at + size:at + 2 * size])

    queries, keys, values = (chosen(w_qkv, kind * 2 * half, half) for kind in range(3))
    out_cols = chosen(w_out, 0, 2 * half)
    out_cols = jnp.concatenate([out_cols[:, :half], out_cols[:, half:]], axis=0)
    payload = jnp.concatenate([keys, values, out_cols, queries], axis=1)
    moved = []
    for step in (1, -1, 2):
        moved.append(spread_z(payload, step))
    piece = jnp.where(is_home, payload, moved[0] + moved[1] + moved[2])

    live_own = live[0].astype(F32)[None]
    marks = jnp.pad(live_own.astype(BF), ((0, 15), (0, model - length)))
    far = across(jnp.concatenate([frames[0], marks], axis=0))
    live_2 = both(core, live_own, swap_core(live_own), 1)
    unit_rows, inverse = norm_rows(frames[0].astype(F32))
    normed = (unit_rows * norm_gain).astype(BF)
    upstream = cotangent[0]
    upstream_other = swap_core(upstream)
    upstream_2 = both(core, upstream, upstream_other, 0)
    normed_other = swap_core(normed)
    normed_2 = both(core, normed, normed_other, 0)
    normed_t = turn(normed_2)
    blocks = ZH * Y
    width = model // (2 * blocks)
    cot_mine = lax.dynamic_index_in_dim(
        upstream_2.reshape(2 * length, ZH, Y, 2, width), core, 3, keepdims=False)
    cot_mine = cot_mine.transpose(0, 2, 1, 3).reshape(2 * length, Y, ZH * width)
    cot_mine = jnp.concatenate([
        cot_mine[:, :, :128].reshape(2 * length, Y * 128),
        cot_mine[:, :, 128:].reshape(2 * length, Y * TAIL)], axis=1)

    spread = jnp.broadcast_to(piece[None], (shards,) + piece.shape)
    weights = lax.all_to_all(spread, ("y", "x"), 0, 0, tiled=True)
    w_kv = weights[:, :, :2 * half].reshape(model, 2 * half)
    pairs = dot(w_kv, normed_2, 0, 1).astype(BF)
    before = along_y(pairs, 1)
    after = along_y(pairs, -1)
    w_o = weights[:, :, 2 * half:3 * half]
    count = shards // 2
    w_o_mine = lax.dynamic_slice_in_dim(w_o, core * count, count, 0)
    w_o_other = swap_core(lax.dynamic_slice_in_dim(w_o, (1 - core) * count, count, 0))
    grad_att = out_grads(flags, w_o_mine, w_o_other, upstream_2, live_2)
    w_q = weights[:, :, 3 * half:].reshape(model, half)
    query = dot(w_q, normed_2, 0, 1).astype(BF)

    far, _ = lax.optimization_barrier((far, pairs))
    far_live = far[length:length + 1, :length].astype(F32)
    far_live = both(core, far_live, swap_core(far_live), 1)
    far = (norm_rows(far[:length].astype(F32))[0] * norm_gain).astype(BF)
    far_2 = both(core, far, swap_core(far), 0)
    beyond = dot(w_kv, far_2, 0, 1).astype(BF)

    live_before = along_y(live_2, 1) + far_live * flags[2].astype(F32)
    live_after = along_y(live_2, -1) + far_live * flags[1].astype(F32)
    span = length + 2 * WIN
    key_pos = jnp.arange(span, dtype=jnp.int32) - WIN
    query_pos = jnp.arange(length, dtype=jnp.int32)
    in_window = jnp.abs(query_pos[None, :] - key_pos[:, None]) <= WIN
    live_all = jnp.concatenate([live_before, live_2, live_after], axis=1)[0]
    bias = jnp.stack([
        jnp.where(in_window & (live_all[i * length:i * length + span, None] > 0.5), 0.0, NEG)
        for i in range(2)
    ])

    pair_shape = (2, half, 2 * length)
    attended, grad_query, grad_own, grad_before, grad_after, grad_far = attention(
        flags, query, grad_att, pairs.reshape(pair_shape), before.reshape(pair_shape),
        after.reshape(pair_shape), beyond.reshape(pair_shape), bias, live_2,
    )
    from_after = along_y(grad_before, -1)
    from_before = along_y(grad_after, 1)
    from_far = across(grad_far)

    attended_other = swap_core(attended)
    grad_query_other = swap_core(grad_query)
    grad_far_other = swap_core(grad_far)
    term_out = out_terms(flags, attended, attended_other, cot_mine)
    far_2, _ = lax.optimization_barrier((far_2, grad_own))
    far_t = turn(far_2)
    grad_own, term_out, far_t = lax.optimization_barrier((grad_own, term_out, far_t))

    grad_pairs = (grad_own + from_after.astype(F32) + from_before.astype(F32)).astype(BF)
    pairs_other = swap_core(grad_pairs)
    terms = weight_terms(flags, normed_t, far_t, (grad_query, grad_query_other), (grad_pairs, pairs_other),
                         (grad_far, grad_far_other), term_out)
    grad_pairs, terms = lax.optimization_barrier((grad_pairs, terms))
    got = lax.all_to_all(terms.reshape((X * Y,) + terms.shape[2:]), ("x", "y"), 0, 0, tiled=True)

    grad_pairs = (grad_pairs.astype(F32) + from_far.astype(F32)).astype(BF).reshape(2 * half, 2 * length)
    part = dot(grad_pairs, w_kv, 0, 1) + dot(grad_query, w_q, 0, 1)
    part = part.reshape(2, length, model)
    part_send = lax.dynamic_index_in_dim(part, 1 - core, 0, keepdims=False).astype(BF)
    part_mine = lax.dynamic_index_in_dim(part, core, 0, keepdims=False)
    grad_unit = (part_mine + swap_core(part_send).astype(F32)) * norm_gain

    sums = jnp.sum(got.astype(F32), axis=0).astype(BF)
    owners = ZL * ZH
    block = shard // 2
    sum_qkv = sums[:owners * shard].reshape(owners, shard, 128)
    sum_out = sums[owners * shard:]
    tails = sum_out[ZL * block:].reshape(block, ZL, TAIL).transpose(1, 0, 2)
    sum_out = jnp.concatenate([sum_out[:ZL * block].reshape(ZL, block, 128), tails], axis=2)
    sum_out = sum_out.reshape(ZL, block, ZH, width).transpose(0, 2, 1, 3).reshape(owners, block, width)
    sum_out = jnp.pad(sum_out, ((0, 0), (0, 0), (0, 128 - width)))
    sums = jnp.concatenate([sum_qkv, sum_out], axis=1)
    sums = lax.all_to_all(sums, ("zl", "zh"), 0, 0, tiled=True)
    factor = 1.0 / math.sqrt(shards * blocks * 2 * length)
    total = jnp.sum(sums.astype(F32), axis=0) * factor

    through = inverse * (
        grad_unit
        - jnp.mean(grad_unit, axis=-1, keepdims=True)
        - unit_rows * jnp.mean(grad_unit * unit_rows, axis=-1, keepdims=True)
    )
    grad_rows = (upstream.astype(F32) + through).astype(BF)[None]
    cols = w_qkv.shape[1] // (2 * blocks)
    return (grad_rows, total[:shard, :cols], total[shard:, :model // (2 * blocks)])


def solution(mesh):
    split = Mesh(mesh.devices.reshape(ZL, X, ZH, Y, C), ("zl", "x", "zh", "y", "c"))
    dp, seq = ("zl", "x"), ("zh", "y", "c")
    return jax.shard_map(
        body,
        mesh=split,
        in_specs=(P(dp, seq, None), P(dp, seq), P(), P(dp, None), P(dp, None), P(dp, seq, None)),
        out_specs=(P(dp, seq, None), P(dp, seq), P(dp, seq)),
        check_vma=False,
    )
```
